32 devices in a mesh: wide: 8 (over z, x), grp: 4 (over y, core).
Axes of the slice: x: 2, y: 2, z: 4, core: 2. Of those that a mesh axis runs over, the one named last changes fastest.
Arguments:
- query_rows: bfloat16 [4096, 1280], P(('wide', 'grp')), may hold values from -9 to 9, as said below
- key_rows: bfloat16 [4096, 1280], P(('wide', 'grp')), may hold values from -9 to 9, as said below
- value_rows: bfloat16 [4096, 1280], P(('wide', 'grp')), may hold values from -6 to 6
- block_image: int32 [32], replicated, may hold values from 0 to 6, never falling along the last dimension, each value on 1 to 8 neighbouring positions
Outputs:
- attended: bfloat16 [4096, 1280], P(('wide', 'grp'))
The draws below stay inside these ranges and needn't reach their ends.
Inputs may be any that keep to these rules, and one draw needn't show every extreme that they name: `query_rows`: Queries: entries bounded as stated. `key_rows`: Keys: entries bounded as stated. `block_image`: image numbers never fall along the window; every image covers 1 to 8 whole blocks and one covers exactly 8.
All inputs are finite; a program needn't handle non-finite values.
Results may differ from the reference program's by a relative error of at most 0.004.
Values may be sent and summed in bfloat16 or wider, within the bound.
A program may use at most 64 MiB of HBM per device.

```python
import math
import jax
import jax.numpy as jnp
import numpy as np
from jax import lax

HEADS = 16
HDIM = 80
BLK = 128
MOST = 8
NBLK = 32
TOKENS = 4096
IMAGES = 7


def plant_pair(key):
    width = HEADS * HDIM
    queries = jnp.clip(1.5 * jax.random.normal(jax.random.fold_in(key, 7), (TOKENS, width)), -9.0, 9.0)
    key_table = jnp.clip(1.5 * jax.random.normal(jax.random.fold_in(key, 8), (TOKENS, width)), -9.0, 9.0)
    return (queries.astype(jnp.float32), key_table.astype(jnp.float32))


def draw_query_rows(key, part):
    return plant_pair(key)[0].astype(jnp.bfloat16)


def draw_key_rows(key, part):
    return plant_pair(key)[1].astype(jnp.bfloat16)


def level_of(own_key, dims, shards, smallest, largest):
    gain, own = 1.0, jax.random.fold_in(own_key, 6)
    for position, shards_of in shards:
        heights = jnp.exp(jax.random.uniform(jax.random.fold_in(own, position), (shards_of,), jnp.float32, smallest / len(shards), largest / len(shards)))
        gain = gain * jnp.repeat(heights, dims[position] // shards_of).reshape([-1 if axis == position else 1 for axis in range(len(dims))])
    return gain


def profile(count, total, limit, lean):
    weights = [(1 << 20) // math.isqrt(standing ** lean) + 1 for standing in range(2, count + 1)]
    rest, holding = total - limit - (count - 1), [1] * (count - 1)
    while rest > 0:
        candidates = [i for i in range(count - 1) if holding[i] < limit]
        whole, remaining = sum([weights[i] for i in candidates]), rest
        for i in candidates:
            addition = min(limit - holding[i], max(1, remaining * weights[i] // whole), rest)
            holding[i] = holding[i] + addition
            rest = rest - addition
    return np.array([limit] + holding)


def uneven(stream_key, amount, total, most, slope):
    if amount == 2:
        one = jax.random.randint(stream_key, (), max(1, total - most), min(most, total - 1) + 1)
        return jnp.stack([one, total - one])
    sizes = jnp.asarray(profile(amount, total, most, slope), jnp.int32)
    twos = (amount - 1) // 2
    giver, sink = sizes[1:1 + 2 * twos:2], sizes[2:2 + 2 * twos:2]
    room = jnp.minimum(giver - 1, most - sink)
    moved = jax.random.randint(jax.random.fold_in(stream_key, 1), (twos,), 0, 1 << 20) % (room + 1)
    sizes = sizes.at[1:1 + 2 * twos:2].set(giver - moved).at[2:2 + 2 * twos:2].set(sink + moved)
    return sizes[jax.random.permutation(jax.random.fold_in(stream_key, 2), amount)]


def bell_draw(own_key, extent, scale, limit, shards=(), held_as=jnp.bfloat16):
    gain = level_of(own_key, extent, shards, -0.22, 0.18) if shards else 1.0
    values = jax.random.normal(own_key, extent, jnp.float32) * scale * gain
    return jnp.minimum(jnp.maximum(values, -limit), limit).astype(held_as)


def setup_inputs(seed: int = 0) -> dict:
    arg_keys = jax.random.split(jax.random.key(seed), 5)
    query_rows = draw_query_rows(jax.random.fold_in(arg_keys[4], 71), 0)
    key_rows = draw_key_rows(jax.random.fold_in(arg_keys[4], 71), 0)
    value_rows = bell_draw(arg_keys[2], (TOKENS, HEADS * HDIM), 1.0, 6.0, ((0, 32),))
    block_image = jnp.searchsorted(jnp.cumsum(uneven(arg_keys[3], IMAGES, NBLK, MOST, 1)), jnp.arange(NBLK), side="right").astype(jnp.int32)
    return {"query_rows": query_rows, "key_rows": key_rows, "value_rows": value_rows, "block_image": block_image}


neg_large = -1e+30

def reference(query_rows, key_rows, value_rows, block_image):
    margin = (MOST - 1) * BLK
    span_rows = BLK + 2 * margin
    token_ids = jnp.broadcast_to(block_image[:, None], (NBLK, BLK)).reshape(-1).astype(jnp.int32)
    padded_ids = jnp.pad(token_ids, (margin, margin), constant_values=-1)
    padded_keys = jnp.pad(key_rows.reshape(TOKENS, HEADS, HDIM), ((margin, margin), (0, 0), (0, 0)))
    padded_values = jnp.pad(value_rows.reshape(TOKENS, HEADS, HDIM), ((margin, margin), (0, 0), (0, 0)))
    query_heads = query_rows.reshape(NBLK, BLK, HEADS, HDIM)
    scale_value = 1.0 / math.sqrt(HDIM)

    def one_block(block_index):
        first_row = (block_index * BLK).astype(jnp.int32)
        query_block = lax.dynamic_index_in_dim(query_heads, block_index, 0, keepdims=False).astype(jnp.float32)
        key_window = lax.dynamic_slice_in_dim(padded_keys, first_row, span_rows, 0).astype(jnp.float32)
        value_window = lax.dynamic_slice_in_dim(padded_values, first_row, span_rows, 0).astype(jnp.float32)
        id_window = lax.dynamic_slice_in_dim(padded_ids, first_row, span_rows, 0)
        query_ids = lax.dynamic_slice_in_dim(token_ids, first_row, BLK, 0)
        same_image = query_ids[:, None] == id_window[None, :]
        scores = jnp.einsum('qhd,khd->hqk', query_block, key_window) * scale_value
        scores = jnp.where(same_image[None], scores, neg_large)
        row_max = lax.optimization_barrier(jnp.max(scores, axis=-1, keepdims=True))
        weights = jnp.where(same_image[None], jnp.exp(scores - row_max), 0.0)
        denominator = lax.optimization_barrier(jnp.sum(weights, axis=-1))
        rounded = lax.optimization_barrier(weights.astype(jnp.bfloat16)).astype(jnp.float32)
        attended = jnp.einsum('hqk,khd->qhd', rounded, value_window) / jnp.transpose(denominator)[:, :, None]
        return attended.reshape(BLK, HEADS * HDIM).astype(jnp.bfloat16)
    blocks = lax.map(one_block, jnp.arange(NBLK, dtype=jnp.int32))
    return blocks.reshape(TOKENS, HEADS * HDIM)
```

```python
import functools
import math

import jax
import jax.numpy as jnp
from jax import lax
from jax.experimental import pallas as pl
from jax.experimental.pallas import tpu as pltpu
from jax.sharding import PartitionSpec as P

HDIM = 80
BLK = 128
MOST = 8
NEG = -1e30
MESH = pl.DeviceIdType.MESH


def kernel(cfg, img, q_in, k_in, v_in, out, kv_src, q_src, kv_own, q_own, halo, kn_own, kn_halo,
           m_scr, l_scr, acc, s_scr, p_scr, o_src, o_own,
           kv_ss, kv_rs, q_ss, q_rs, up_ss, dn_ss, halo_rs, o_ss, o_rs, loc_s):
    planes, fold, grp, heads = cfg
    n = fold * grp
    cols = heads * HDIM
    wide_at, grp_at = lax.axis_index("wide"), lax.axis_index("grp")
    plane = wide_at // fold
    fold_at = wide_at % fold
    me = fold_at * grp + grp_at
    has_prev, has_next = plane > 0, plane < planes - 1

    def device(at_plane, member):
        return (at_plane * fold + member // grp, member % grp)

    offsets = [(a, b) for a in range(fold) for b in range(grp)][1:]

    def to_peer(a, b):
        return ((fold_at + a) % fold) * grp + (grp_at + b) % grp

    def from_peer(a, b):
        return ((fold_at + fold - a) % fold) * grp + (grp_at + grp - b) % grp

    barrier = pltpu.get_barrier_semaphore()
    for a, b in offsets:
        pl.semaphore_signal(barrier, inc=1, device_id=device(plane, to_peer(a, b)), device_id_type=MESH)

    @pl.when(has_prev)
    def _():
        pl.semaphore_signal(barrier, inc=1, device_id=device(plane - 1, me), device_id_type=MESH)

    @pl.when(has_next)
    def _():
        pl.semaphore_signal(barrier, inc=1, device_id=device(plane + 1, me), device_id_type=MESH)

    def turn(ref, store):
        whole = jnp.concatenate([ref[:, c:c + BLK].T for c in range(0, n * cols, BLK)], axis=0)
        for member in range(n):
            store(member, whole[member * cols:(member + 1) * cols])

    def put_k(member, x):
        kv_src[member, 0] = x

    def put_v(member, x):
        kv_src[member, 1] = x

    def put_q(member, x):
        q_src[member] = x

    turn(k_in, put_k)
    turn(v_in, put_v)
    turn(q_in, put_q)

    @pl.when(jnp.logical_not(has_prev))
    def _():
        halo[0:n] = jnp.zeros((n,) + halo.shape[1:], halo.dtype)

    @pl.when(jnp.logical_not(has_next))
    def _():
        halo[n:2 * n] = jnp.zeros((n,) + halo.shape[1:], halo.dtype)

    pl.semaphore_wait(barrier, n - 1 + has_prev.astype(jnp.int32) + has_next.astype(jnp.int32))

    def remote(src, dst, ss, rs, dev):
        return pltpu.make_async_remote_copy(src_ref=src, dst_ref=dst, send_sem=ss, recv_sem=rs,
                                            device_id=dev, device_id_type=MESH)

    def up(member, src):
        return remote(src, halo.at[member], up_ss.at[member], halo_rs.at[member], device(plane + 1, me))

    def down(member, src):
        return remote(src, halo.at[n + member], dn_ss.at[member], halo_rs.at[n + member], device(plane - 1, me))

    def forward(member, src):
        @pl.when(jnp.logical_and(has_next, member >= 1))
        def _():
            up(member, src).start()

        @pl.when(jnp.logical_and(has_prev, member <= n - 2))
        def _():
            down(member, src).start()

    def kv_copy(src, dst):
        return remote(kv_src.at[dst], kv_own.at[src], kv_ss.at[dst], kv_rs.at[src], device(plane, dst))

    def q_copy(src, dst):
        return remote(q_src.at[dst], q_own.at[src], q_ss.at[dst], q_rs.at[src], device(plane, dst))

    forward(me, kv_src.at[me])
    for a, b in offsets:
        kv_copy(me, to_peer(a, b)).start()
    for a, b in offsets:
        q_copy(me, to_peer(a, b)).start()
    keep_kv = pltpu.make_async_copy(kv_src.at[me], kv_own.at[me], loc_s.at[0])
    keep_q = pltpu.make_async_copy(q_src.at[me], q_own.at[me], loc_s.at[1])
    keep_kv.start()
    keep_q.start()
    for a, b in offsets:
        source = from_peer(a, b)
        kv_copy(source, me).wait_recv()
        forward(source, kv_own.at[source])
    keep_kv.wait()
    keep_q.wait()

    def natural(src, dst):
        for h in range(heads):
            dst[h] = src[h * HDIM:(h + 1) * HDIM].T

    @pl.loop(0, n)
    def _(b):
        natural(kv_own.at[b, 0], kn_own.at[b])

    for a, b in offsets:
        q_copy(from_peer(a, b), me).wait_recv()

    factor = math.log2(math.e) / math.sqrt(HDIM)
    blocks = img.shape[0]
    lane = lax.broadcasted_iota(jnp.int32, (1, 2 * BLK), 1)
    base = plane * n

    def live_row(first, key_block):
        inside = jnp.logical_and(key_block >= 0, key_block < blocks)
        key_id = img[jnp.clip(key_block, 0, blocks - 1)]
        key_id = jnp.where(inside, key_id, -2)
        ids = jnp.where(lane < BLK, img[first], img[first + 1])
        return ids == key_id

    def scores_and_max(h, pair, keys, live, start):
        q_pair = jnp.concatenate([q_own[2 * pair, pl.ds(h * HDIM, HDIM)],
                                  q_own[2 * pair + 1, pl.ds(h * HDIM, HDIM)]], axis=1)
        top = start
        for t in range(n):
            s = jnp.dot(keys(t), q_pair, preferred_element_type=jnp.float32)
            s_scr[t] = s
            top = jnp.maximum(top, jnp.where(live[t], jnp.max(s, axis=0, keepdims=True), NEG))
        return top

    def weigh(top, live, values):
        total = jnp.zeros((8, 2 * BLK), jnp.float32)
        for t in range(n):
            shift = jnp.where(live[t], -top * factor, NEG)
            w = jnp.exp2(s_scr[t] * factor + shift)
            total = total + jnp.sum(w.reshape(BLK // 8, 8, 2 * BLK), axis=0)
            p_scr[t * BLK:(t + 1) * BLK] = w.astype(jnp.bfloat16)
        v = jnp.concatenate([values(t) for t in range(n)], axis=1)
        out_t = jnp.dot(v, p_scr[...], preferred_element_type=jnp.float32)
        return out_t, jnp.sum(total, axis=0, keepdims=True)

    def near(step, carry):
        pair = step
        first = base + 2 * pair
        live = [live_row(first, base + t) for t in range(n)]
        for h in range(heads):
            top = scores_and_max(h, pair, lambda t: kn_own[t, h], live, jnp.full((1, 2 * BLK), NEG, jnp.float32))
            out_t, total = weigh(top, live, lambda t: kv_own[t, 1, h * HDIM:(h + 1) * HDIM])
            m_scr[pair * heads + h] = top
            l_scr[pair * heads + h] = total
            acc[pair * heads + h] = out_t
        return carry

    lax.fori_loop(0, n // 2, near, 0)

    for member in range(1, n):
        @pl.when(has_prev)
        def _():
            up(member, kv_own.at[member]).wait_recv()
        natural(halo.at[member, 0], kn_halo.at[member])
    for member in range(n - 1):
        @pl.when(has_next)
        def _():
            down(member, kv_own.at[member]).wait_recv()
        natural(halo.at[n + member, 0], kn_halo.at[n + member])

    def out_copy(src, dst):
        return remote(o_src.at[dst], o_own.at[src], o_ss.at[dst], o_rs.at[src], device(plane, dst))

    def far(step, carry):
        pair = (me // 2 + 1 + step) % (n // 2)
        first = base + 2 * pair
        live = []
        for t in range(n):
            slot = 2 * pair + 1 + t
            live.append(live_row(first, jnp.where(slot < n, base - n + slot, base + slot)))
        for h in range(heads):
            at = pair * heads + h
            top1 = m_scr[at]
            top = scores_and_max(h, pair, lambda t: kn_halo[2 * pair + 1 + t, h], live, top1)
            out_t, total = weigh(top, live, lambda t: halo[2 * pair + 1 + t, 1, h * HDIM:(h + 1) * HDIM])
            fade = jnp.exp2((top1 - top) * factor)
            res = (acc[at] * fade + out_t) / (l_scr[at] * fade + total)
            res = res.astype(jnp.bfloat16)
            o_src[2 * pair, h * HDIM:(h + 1) * HDIM] = res[:, :BLK]
            o_src[2 * pair + 1, h * HDIM:(h + 1) * HDIM] = res[:, BLK:]
        for r in range(2):
            dst = 2 * pair + r

            @pl.when(dst != me)
            def _():
                out_copy(me, dst).start()

            @pl.when(dst == me)
            def _():
                pltpu.make_async_copy(o_src.at[me], o_own.at[me], loc_s.at[2]).start()
        return carry

    lax.fori_loop(0, n // 2, far, 0)

    pltpu.make_async_copy(o_src.at[me], o_own.at[me], loc_s.at[2]).wait()
    for a, b in offsets:
        out_copy(from_peer(a, b), me).wait_recv()
    flat = jnp.concatenate([o_own[member] for member in range(n)], axis=0)
    for c in range(0, n * cols, BLK):
        out[:, c:c + BLK] = flat[c:c + BLK].T

    for a, b in offsets:
        kv_copy(me, to_peer(a, b)).wait_send()
        q_copy(me, to_peer(a, b)).wait_send()
        out_copy(me, to_peer(a, b)).wait_send()

    @pl.when(has_next)
    def _():
        for member in range(1, n):
            up(member, kv_own.at[member]).wait_send()

    @pl.when(has_prev)
    def _():
        for member in range(n - 1):
            down(member, kv_own.at[member]).wait_send()


def solution(mesh):
    wide, grp = mesh.shape["wide"], mesh.shape["grp"]
    fold = MOST // grp
    n = fold * grp
    planes = wide // fold

    def body(query_rows, key_rows, value_rows, block_image):
        rows, width = query_rows.shape
        heads = width // HDIM // n
        cols = heads * HDIM
        bf, f32 = jnp.bfloat16, jnp.float32
        vmem = pl.BlockSpec(memory_space=pltpu.VMEM)
        dma = pltpu.SemaphoreType.DMA
        return pl.pallas_call(
            functools.partial(kernel, (planes, fold, grp, heads)),
            out_shape=jax.ShapeDtypeStruct((rows, width), bf),
            in_specs=[pl.BlockSpec(memory_space=pltpu.SMEM), vmem, vmem, vmem],
            out_specs=vmem,
            scratch_shapes=[
                pltpu.VMEM((n, 2, cols, BLK), bf),
                pltpu.VMEM((n, cols, BLK), bf),
                pltpu.VMEM((n, 2, cols, BLK), bf),
                pltpu.VMEM((n, cols, BLK), bf),
                pltpu.VMEM((2 * n, 2, cols, BLK), bf),
                pltpu.VMEM((n, heads, BLK, HDIM), bf),
                pltpu.VMEM((2 * n, heads, BLK, HDIM), bf),
                pltpu.VMEM((n // 2 * heads, 1, 2 * BLK), f32),
                pltpu.VMEM((n // 2 * heads, 1, 2 * BLK), f32),
                pltpu.VMEM((n // 2 * heads, HDIM, 2 * BLK), f32),
                pltpu.VMEM((n, BLK, 2 * BLK), f32),
                pltpu.VMEM((n * BLK, 2 * BLK), bf),
                pltpu.VMEM((n, cols, BLK), bf),
                pltpu.VMEM((n, cols, BLK), bf),
                dma((n,)), dma((n,)), dma((n,)), dma((n,)),
                dma((n,)), dma((n,)), dma((2 * n,)),
                dma((n,)), dma((n,)), dma((3,)),
            ],
            compiler_params=pltpu.CompilerParams(collective_id=0, has_side_effects=True),
        )(block_image, query_rows, key_rows, value_rows)

    return jax.shard_map(
        body,
        mesh=mesh,
        in_specs=(
            P(("wide", "grp"), None),
            P(("wide", "grp"), None),
            P(("wide", "grp"), None),
            P(),
        ),
        out_specs=P(("wide", "grp"), None),
        check_vma=False,
    )
```

```python
import functools
import math

import jax
import jax.numpy as jnp
from jax import lax
from jax.experimental import pallas as pl
from jax.experimental.pallas import tpu as pltpu
from jax.sharding import PartitionSpec as P

HDIM = 80
BLK = 128
MOST = 8
NEG = -1e30
MESH = pl.DeviceIdType.MESH


def kernel(cfg, img, q_hbm, k_hbm, v_hbm, out, q_in, k_in, v_in, k_src, q_src, v_src, k_own, q_own, v_own,
           k_halo, v_halo, kn_own, kn_halo, m_scr, l_scr, acc, s_scr, p_near, p_far, o_src, o_own,
           k_ss, k_rs, q_ss, q_rs, v_ss, v_rs, k_up, k_dn, k_hr, v_up, v_dn, v_hr, o_ss, o_rs, loc_s):
    planes, fold, grp, heads = cfg
    n = fold * grp
    cols = heads * HDIM
    wide_at, grp_at = lax.axis_index("wide"), lax.axis_index("grp")
    plane = wide_at // fold
    fold_at = wide_at % fold
    me = fold_at * grp + grp_at
    has_prev, has_next = plane > 0, plane < planes - 1

    loads = [pltpu.make_async_copy(src, dst, loc_s.at[i])
             for i, (src, dst) in enumerate(((k_hbm, k_in), (q_hbm, q_in), (v_hbm, v_in)))]
    for load in loads:
        load.start()

    def device(at_plane, member):
        return (at_plane * fold + member // grp, member % grp)

    def to_peer(i):
        return ((fold_at + i // grp) % fold) * grp + (grp_at + i % grp) % grp

    def from_peer(i):
        return ((fold_at + fold - i // grp) % fold) * grp + (grp_at + grp - i % grp) % grp

    barrier = pltpu.get_barrier_semaphore()
    for i in range(1, n):
        pl.semaphore_signal(barrier, inc=1, device_id=device(plane, to_peer(i)), device_id_type=MESH)

    @pl.when(has_prev)
    def _():
        pl.semaphore_signal(barrier, inc=1, device_id=device(plane - 1, me), device_id_type=MESH)

    @pl.when(has_next)
    def _():
        pl.semaphore_signal(barrier, inc=1, device_id=device(plane + 1, me), device_id_type=MESH)

    def turn(ref, dst):
        whole = jnp.concatenate([ref[:, c:c + BLK].T for c in range(0, n * cols, BLK)], axis=0)
        for member in range(n):
            dst[member] = whole[member * cols:(member + 1) * cols]

    @pl.when(jnp.logical_not(has_prev))
    def _():
        for ref in (k_halo, v_halo):
            ref[0:n] = jnp.zeros((n,) + ref.shape[1:], ref.dtype)

    @pl.when(jnp.logical_not(has_next))
    def _():
        for ref in (k_halo, v_halo):
            ref[n:2 * n] = jnp.zeros((n,) + ref.shape[1:], ref.dtype)

    for load, ref, dst in zip(loads, (k_in, q_in, v_in), (k_src, q_src, v_src)):
        load.wait()
        turn(ref, dst)

    pl.semaphore_wait(barrier, n - 1 + has_prev.astype(jnp.int32) + has_next.astype(jnp.int32))

    def remote(src, dst, ss, rs, dev):
        return pltpu.make_async_remote_copy(src_ref=src, dst_ref=dst, send_sem=ss, recv_sem=rs,
                                            device_id=dev, device_id_type=MESH)

    k_halos, v_halos = (k_halo, k_up, k_dn, k_hr), (v_halo, v_up, v_dn, v_hr)

    def up(halos, member, src):
        halo, ss, _, rs = halos
        return remote(src, halo.at[member], ss.at[member], rs.at[member], device(plane + 1, me))

    def down(halos, member, src):
        halo, _, ss, rs = halos
        return remote(src, halo.at[n + member], ss.at[member], rs.at[n + member], device(plane - 1, me))

    def forward(halos, member, src):
        @pl.when(jnp.logical_and(has_next, member >= 1))
        def _():
            up(halos, member, src).start()

        @pl.when(jnp.logical_and(has_prev, member <= n - 2))
        def _():
            down(halos, member, src).start()

    def k_copy(src, dst):
        return remote(k_src.at[dst], k_own.at[src], k_ss.at[dst], k_rs.at[src], device(plane, dst))

    def q_copy(src, dst):
        return remote(q_src.at[dst], q_own.at[src], q_ss.at[dst], q_rs.at[src], device(plane, dst))

    def v_copy(src, dst):
        return remote(v_src.at[dst], v_own.at[src], v_ss.at[dst], v_rs.at[src], device(plane, dst))

    forward(k_halos, me, k_src.at[me])
    for copy in (k_copy, q_copy, v_copy):
        for i in range(1, n):
            copy(me, to_peer(i)).start()
    forward(v_halos, me, v_src.at[me])
    keeps = [pltpu.make_async_copy(src.at[me], dst.at[me], loc_s.at[i])
             for i, (src, dst) in enumerate(((k_src, k_own), (q_src, q_own), (v_src, v_own)))]
    for keep in keeps:
        keep.start()

    def natural(src, dst):
        for h in range(heads):
            dst[h] = src[h * HDIM:(h + 1) * HDIM].T

    keeps[0].wait()
    natural(k_own.at[me], kn_own.at[me])

    def take_k(i, carry):
        source = from_peer(i)
        k_copy(source, me).wait_recv()
        forward(k_halos, source, k_own.at[source])
        natural(k_own.at[source], kn_own.at[source])
        return carry

    lax.fori_loop(1, n, take_k, 0)
    for keep in keeps[1:]:
        keep.wait()
    for i in range(1, n):
        q_copy(from_peer(i), me).wait_recv()

    factor = math.log2(math.e) / math.sqrt(HDIM)
    blocks = img.shape[0]
    lane = lax.broadcasted_iota(jnp.int32, (1, 2 * BLK), 1)
    base = plane * n
    pairs = n // 2

    def live_row(first, key_block):
        inside = jnp.logical_and(key_block >= 0, key_block < blocks)
        key_id = img[jnp.clip(key_block, 0, blocks - 1)]
        key_id = jnp.where(inside, key_id, -2)
        ids = jnp.where(lane < BLK, img[first], img[first + 1])
        return ids == key_id

    def weights(h, pair, keys, live, start, p_dst):
        q_pair = jnp.concatenate([q_own[2 * pair, pl.ds(h * HDIM, HDIM)],
                                  q_own[2 * pair + 1, pl.ds(h * HDIM, HDIM)]], axis=1)
        top = start
        for t in range(n):
            s = jnp.dot(keys(t), q_pair, preferred_element_type=jnp.float32)
            s_scr[h, t] = s
            top = jnp.maximum(top, jnp.where(live[t], jnp.max(s, axis=0, keepdims=True), NEG))
        total = jnp.zeros((8, 2 * BLK), jnp.float32)
        for t in range(n):
            shift = jnp.where(live[t], -top * factor, NEG)
            w = jnp.exp2(s_scr[h, t] * factor + shift)
            total = total + jnp.sum(w.reshape(BLK // 8, 8, 2 * BLK), axis=0)
            p_dst[t * BLK:(t + 1) * BLK] = w.astype(jnp.bfloat16)
        return top, jnp.sum(total, axis=0, keepdims=True)

    def times(values, p_src):
        v = jnp.concatenate([values(t) for t in range(n)], axis=1)
        return jnp.dot(v, p_src[...], preferred_element_type=jnp.float32)

    def take_v(i):
        source = from_peer(i)
        v_copy(source, me).wait_recv()
        forward(v_halos, source, v_own.at[source])

    def near(pair, carry):
        first = base + 2 * pair
        live = [live_row(first, base + t) for t in range(n)]
        for h in range(heads):
            at = pair * heads + h
            m_scr[at], l_scr[at] = weights(h, pair, lambda t: kn_own[t, h], live,
                                           jnp.full((1, 2 * BLK), NEG, jnp.float32), p_near.at[at])
        take_v(2 * pair + 1)

        @pl.when(pair < pairs - 1)
        def _():
            take_v(2 * pair + 2)
        return carry

    lax.fori_loop(0, pairs, near, 0)

    def take_halo(halos, src):
        @pl.when(has_prev)
        def _():
            for member in range(1, n):
                up(halos, member, src.at[member]).wait_recv()

        @pl.when(has_next)
        def _():
            for member in range(n - 1):
                down(halos, member, src.at[member]).wait_recv()

    take_halo(k_halos, k_own)

    def turn_halo(slot, carry):
        natural(k_halo.at[slot], kn_halo.at[slot])
        return carry

    lax.fori_loop(1, 2 * n - 1, turn_halo, 0)

    def far(pair, carry):
        first = base + 2 * pair
        live = []
        for t in range(n):
            slot = 2 * pair + 1 + t
            live.append(live_row(first, jnp.where(slot < n, base - n + slot, base + slot)))
        for h in range(heads):
            at = pair * heads + h
            top1 = m_scr[at]
            top, total = weights(h, pair, lambda t: kn_halo[2 * pair + 1 + t, h], live, top1, p_far.at[at])
            fade = jnp.exp2((top1 - top) * factor)
            out_t = times(lambda t: v_own[t, h * HDIM:(h + 1) * HDIM], p_near.at[at])
            acc[at] = out_t * fade
            l_scr[at] = l_scr[at] * fade + total
        return carry

    lax.fori_loop(0, pairs, far, 0)
    take_halo(v_halos, v_own)

    def out_copy(src, dst):
        return remote(o_src.at[dst], o_own.at[src], o_ss.at[dst], o_rs.at[src], device(plane, dst))

    def finish(step, carry):
        pair = (me // 2 + 1 + step) % pairs
        for h in range(heads):
            at = pair * heads + h
            out_t = times(lambda t: v_halo[2 * pair + 1 + t, h * HDIM:(h + 1) * HDIM], p_far.at[at])
            res = ((acc[at] + out_t) / l_scr[at]).astype(jnp.bfloat16)
            o_src[2 * pair, h * HDIM:(h + 1) * HDIM] = res[:, :BLK]
            o_src[2 * pair + 1, h * HDIM:(h + 1) * HDIM] = res[:, BLK:]
        for r in range(2):
            dst = 2 * pair + r

            @pl.when(dst != me)
            def _():
                out_copy(me, dst).start()

            @pl.when(dst == me)
            def _():
                pltpu.make_async_copy(o_src.at[me], o_own.at[me], loc_s.at[0]).start()
        return carry

    lax.fori_loop(0, pairs, finish, 0)

    pltpu.make_async_copy(o_src.at[me], o_own.at[me], loc_s.at[0]).wait()
    for i in range(1, n):
        out_copy(from_peer(i), me).wait_recv()
    flat = jnp.concatenate([o_own[member] for member in range(n)], axis=0)
    for c in range(0, n * cols, BLK):
        out[:, c:c + BLK] = flat[c:c + BLK].T

    for copy in (k_copy, q_copy, v_copy, out_copy):
        for i in range(1, n):
            copy(me, to_peer(i)).wait_send()

    for halos, src in ((k_halos, k_own), (v_halos, v_own)):
        @pl.when(has_next)
        def _():
            for member in range(1, n):
                up(halos, member, src.at[member]).wait_send()

        @pl.when(has_prev)
        def _():
            for member in range(n - 1):
                down(halos, member, src.at[member]).wait_send()


def solution(mesh):
    wide, grp = mesh.shape["wide"], mesh.shape["grp"]
    fold = MOST // grp
    n = fold * grp
    planes = wide // fold

    def body(query_rows, key_rows, value_rows, block_image):
        rows, width = query_rows.shape
        heads = width // HDIM // n
        cols = heads * HDIM
        bf, f32 = jnp.bfloat16, jnp.float32
        vmem = pl.BlockSpec(memory_space=pltpu.VMEM)
        hbm = pl.BlockSpec(memory_space=pl.ANY)
        dma = pltpu.SemaphoreType.DMA
        units = n // 2 * heads
        slices = pltpu.VMEM((n, cols, BLK), bf)
        return pl.pallas_call(
            functools.partial(kernel, (planes, fold, grp, heads)),
            out_shape=jax.ShapeDtypeStruct((rows, width), bf),
            in_specs=[pl.BlockSpec(memory_space=pltpu.SMEM), hbm, hbm, hbm],
            out_specs=vmem,
            scratch_shapes=[pltpu.VMEM((rows, width), bf)] * 3 + [slices] * 6 + [
                pltpu.VMEM((2 * n, cols, BLK), bf),
                pltpu.VMEM((2 * n, cols, BLK), bf),
                pltpu.VMEM((n, heads, BLK, HDIM), bf),
                pltpu.VMEM((2 * n, heads, BLK, HDIM), bf),
                pltpu.VMEM((units, 1, 2 * BLK), f32),
                pltpu.VMEM((units, 1, 2 * BLK), f32),
                pltpu.VMEM((units, HDIM, 2 * BLK), f32),
                pltpu.VMEM((heads, n, BLK, 2 * BLK), f32),
                pltpu.VMEM((units, n * BLK, 2 * BLK), bf),
                pltpu.VMEM((units, n * BLK, 2 * BLK), bf),
                slices, slices,
            ] + [dma((n,))] * 6 + [dma((n,)), dma((n,)), dma((2 * n,))] * 2 + [dma((n,)), dma((n,)), dma((3,))],
            compiler_params=pltpu.CompilerParams(collective_id=0, has_side_effects=True),
        )(block_image, query_rows, key_rows, value_rows)

    return jax.shard_map(
        body,
        mesh=mesh,
        in_specs=(
            P(("wide", "grp"), None),
            P(("wide", "grp"), None),
            P(("wide", "grp"), None),
            P(),
        ),
        out_specs=P(("wide", "grp"), None),
        check_vma=False,
    )
```

```python
import functools
import math

import jax
import jax.numpy as jnp
from jax import lax
from jax.experimental import pallas as pl
from jax.experimental.pallas import tpu as pltpu
from jax.sharding import PartitionSpec as P

HDIM = 80
BLK = 128
MOST = 8
NEG = -1e30
EARLY = 4
MESH = pl.DeviceIdType.MESH


def kernel(cfg, img, q_hbm, k_hbm, v_hbm, out, q_in, k_in, v_in, k_src, q_src, v_src, k_own, q_own, v_own,
           k_halo, v_halo, kn_own, kn_halo, m_scr, l_scr, acc, s_scr, p_near, p_far, o_src, o_own,
           k_ss, k_rs, q_ss, q_rs, v_ss, v_rs, k_up, k_dn, k_hr, v_up, v_dn, v_hr, o_ss, o_rs, loc_s):
    planes, fold, grp, heads = cfg
    n = fold * grp
    cols = heads * HDIM
    wide_at, grp_at = lax.axis_index("wide"), lax.axis_index("grp")
    plane = wide_at // fold
    fold_at = wide_at % fold
    me = fold_at * grp + grp_at
    has_prev, has_next = plane > 0, plane < planes - 1

    loads = [pltpu.make_async_copy(src, dst, loc_s.at[i])
             for i, (src, dst) in enumerate(((k_hbm, k_in), (q_hbm, q_in), (v_hbm, v_in)))]
    for load in loads:
        load.start()

    def device(at_plane, member):
        return (at_plane * fold + member // grp, member % grp)

    def turn_of(j):
        return j % 2 * (n // 2 + j // 2) + (1 - j % 2) * (j // 2)

    def to_peer(j):
        i = turn_of(j)
        return ((fold_at + i // grp) % fold) * grp + (grp_at + i % grp) % grp

    def from_peer(j):
        i = turn_of(j)
        return ((fold_at + fold - i // grp) % fold) * grp + (grp_at + grp - i % grp) % grp

    barrier = pltpu.get_barrier_semaphore()
    for i in range(1, n):
        pl.semaphore_signal(barrier, inc=1, device_id=device(plane, to_peer(i)), device_id_type=MESH)

    @pl.when(has_prev)
    def _():
        pl.semaphore_signal(barrier, inc=1, device_id=device(plane - 1, me), device_id_type=MESH)

    @pl.when(has_next)
    def _():
        pl.semaphore_signal(barrier, inc=1, device_id=device(plane + 1, me), device_id_type=MESH)

    def turn(ref, dst):
        whole = jnp.concatenate([ref[:, c:c + BLK].T for c in range(0, n * cols, BLK)], axis=0)
        for member in range(n):
            dst[member] = whole[member * cols:(member + 1) * cols]

    @pl.when(jnp.logical_not(has_prev))
    def _():
        for ref in (k_halo, v_halo):
            ref[0:n] = jnp.zeros((n,) + ref.shape[1:], ref.dtype)

    @pl.when(jnp.logical_not(has_next))
    def _():
        for ref in (k_halo, v_halo):
            ref[n:2 * n] = jnp.zeros((n,) + ref.shape[1:], ref.dtype)

    for load, ref, dst in zip(loads, (k_in, q_in, v_in), (k_src, q_src, v_src)):
        load.wait()
        turn(ref, dst)

    pl.semaphore_wait(barrier, n - 1 + has_prev.astype(jnp.int32) + has_next.astype(jnp.int32))

    def remote(src, dst, ss, rs, dev):
        return pltpu.make_async_remote_copy(src_ref=src, dst_ref=dst, send_sem=ss, recv_sem=rs,
                                            device_id=dev, device_id_type=MESH)

    k_halos, v_halos = (k_halo, k_up, k_dn, k_hr), (v_halo, v_up, v_dn, v_hr)

    def up(halos, member, src):
        halo, ss, _, rs = halos
        return remote(src, halo.at[member], ss.at[member], rs.at[member], device(plane + 1, me))

    def down(halos, member, src):
        halo, _, ss, rs = halos
        return remote(src, halo.at[n + member], ss.at[member], rs.at[n + member], device(plane - 1, me))

    def forward(halos, member, src):
        @pl.when(jnp.logical_and(has_next, member >= 1))
        def _():
            up(halos, member, src).start()

        @pl.when(jnp.logical_and(has_prev, member <= n - 2))
        def _():
            down(halos, member, src).start()

    def k_copy(src, dst):
        return remote(k_src.at[dst], k_own.at[src], k_ss.at[dst], k_rs.at[src], device(plane, dst))

    def q_copy(src, dst):
        return remote(q_src.at[dst], q_own.at[src], q_ss.at[dst], q_rs.at[src], device(plane, dst))

    def v_copy(src, dst):
        return remote(v_src.at[dst], v_own.at[src], v_ss.at[dst], v_rs.at[src], device(plane, dst))

    forward(k_halos, me, k_src.at[me])
    for i in range(1, n):
        k_copy(me, to_peer(i)).start()
    for i in range(1, EARLY + 1):
        v_copy(me, to_peer(i)).start()
    q_copy(me, me // 2 * 2 + 1 - me % 2).start()
    for step in range(1, n // 2):
        for r in range(2):
            q_copy(me, (me // 2 + n // 2 - step) % (n // 2) * 2 + r).start()
    for i in range(EARLY + 1, n):
        v_copy(me, to_peer(i)).start()
    forward(v_halos, me, v_src.at[me])
    keeps = [pltpu.make_async_copy(src.at[me], dst.at[me], loc_s.at[i])
             for i, (src, dst) in enumerate(((k_src, k_own), (q_src, q_own), (v_src, v_own)))]
    for keep in keeps:
        keep.start()

    def natural(src, dst):
        for h in range(heads):
            dst[h] = src[h * HDIM:(h + 1) * HDIM].T

    keeps[0].wait()
    natural(k_own.at[me], kn_own.at[me])

    def take_k(i, carry):
        source = from_peer(i)
        k_copy(source, me).wait_recv()
        forward(k_halos, source, k_own.at[source])
        natural(k_own.at[source], kn_own.at[source])
        return carry

    lax.fori_loop(1, n, take_k, 0)
    for keep in keeps[1:]:
        keep.wait()
    def take_v(i):
        source = from_peer(i)
        v_copy(source, me).wait_recv()
        forward(v_halos, source, v_own.at[source])

    for i in range(1, EARLY + 1):
        take_v(i)
    factor = math.log2(math.e) / math.sqrt(HDIM)
    blocks = img.shape[0]
    lane = lax.broadcasted_iota(jnp.int32, (1, 2 * BLK), 1)
    base = plane * n
    pairs = n // 2

    def live_row(first, key_block):
        inside = jnp.logical_and(key_block >= 0, key_block < blocks)
        key_id = img[jnp.clip(key_block, 0, blocks - 1)]
        key_id = jnp.where(inside, key_id, -2)
        ids = jnp.where(lane < BLK, img[first], img[first + 1])
        return ids == key_id

    def weights(h, pair, keys, live, start, p_dst):
        q_pair = jnp.concatenate([q_own[2 * pair, pl.ds(h * HDIM, HDIM)],
                                  q_own[2 * pair + 1, pl.ds(h * HDIM, HDIM)]], axis=1)
        top = start
        for t in range(n):
            s = jnp.dot(keys(t), q_pair, preferred_element_type=jnp.float32)
            s_scr[h, t] = s
            top = jnp.maximum(top, jnp.where(live[t], jnp.max(s, axis=0, keepdims=True), NEG))
        total = jnp.zeros((8, 2 * BLK), jnp.float32)
        for t in range(n):
            shift = jnp.where(live[t], -top * factor, NEG)
            w = jnp.exp2(s_scr[h, t] * factor + shift)
            total = total + jnp.sum(w.reshape(BLK // 8, 8, 2 * BLK), axis=0)
            p_dst[t * BLK:(t + 1) * BLK] = w.astype(jnp.bfloat16)
        return top, jnp.sum(total, axis=0, keepdims=True)

    def times(values, p_src):
        v = jnp.concatenate([values(t) for t in range(n)], axis=1)
        return jnp.dot(v, p_src[...], preferred_element_type=jnp.float32)

    def near(step, carry):
        pair = (me // 2 + step) % pairs
        for r in range(2):
            @pl.when(2 * pair + r != me)
            def _():
                q_copy(2 * pair + r, me).wait_recv()
        first = base + 2 * pair
        live = [live_row(first, base + t) for t in range(n)]
        for h in range(heads):
            at = pair * heads + h
            m_scr[at], l_scr[at] = weights(h, pair, lambda t: kn_own[t, h], live,
                                           jnp.full((1, 2 * BLK), NEG, jnp.float32), p_near.at[at])
        return carry

    lax.fori_loop(0, pairs, near, 0)

    def take_halo(halos, src):
        @pl.when(has_prev)
        def _():
            for member in range(1, n):
                up(halos, member, src.at[member]).wait_recv()

        @pl.when(has_next)
        def _():
            for member in range(n - 1):
                down(halos, member, src.at[member]).wait_recv()

    take_halo(k_halos, k_own)

    def turn_halo(slot, carry):
        natural(k_halo.at[slot], kn_halo.at[slot])
        return carry

    cuts = [1 + (2 * n - 2) * i // (n - 1 - EARLY) for i in range(n - EARLY)]
    for i in range(EARLY + 1, n):
        take_v(i)
        lax.fori_loop(cuts[i - EARLY - 1], cuts[i - EARLY], turn_halo, 0)

    def far(pair, carry):
        first = base + 2 * pair
        live = []
        for t in range(n):
            slot = 2 * pair + 1 + t
            live.append(live_row(first, jnp.where(slot < n, base - n + slot, base + slot)))
        for h in range(heads):
            at = pair * heads + h
            top1 = m_scr[at]
            top, total = weights(h, pair, lambda t: kn_halo[2 * pair + 1 + t, h], live, top1, p_far.at[at])
            fade = jnp.exp2((top1 - top) * factor)
            out_t = times(lambda t: v_own[t, h * HDIM:(h + 1) * HDIM], p_near.at[at])
            acc[at] = out_t * fade
            l_scr[at] = l_scr[at] * fade + total
        return carry

    lax.fori_loop(0, pairs, far, 0)
    take_halo(v_halos, v_own)

    def out_copy(src, dst):
        return remote(o_src.at[dst], o_own.at[src], o_ss.at[dst], o_rs.at[src], device(plane, dst))

    def finish(step, carry):
        pair = (me // 2 + 1 + step) % pairs
        for h in range(heads):
            at = pair * heads + h
            out_t = times(lambda t: v_halo[2 * pair + 1 + t, h * HDIM:(h + 1) * HDIM], p_far.at[at])
            res = ((acc[at] + out_t) / l_scr[at]).astype(jnp.bfloat16)
            o_src[2 * pair, h * HDIM:(h + 1) * HDIM] = res[:, :BLK]
            o_src[2 * pair + 1, h * HDIM:(h + 1) * HDIM] = res[:, BLK:]
        for r in range(2):
            dst = 2 * pair + r

            @pl.when(dst != me)
            def _():
                out_copy(me, dst).start()

            @pl.when(dst == me)
            def _():
                pltpu.make_async_copy(o_src.at[me], o_own.at[me], loc_s.at[0]).start()
        return carry

    lax.fori_loop(0, pairs, finish, 0)

    pltpu.make_async_copy(o_src.at[me], o_own.at[me], loc_s.at[0]).wait()
    for i in range(1, n):
        out_copy(from_peer(i), me).wait_recv()
    flat = jnp.concatenate([o_own[member] for member in range(n)], axis=0)
    for c in range(0, n * cols, BLK):
        out[:, c:c + BLK] = flat[c:c + BLK].T

    for copy in (k_copy, q_copy, v_copy, out_copy):
        for i in range(1, n):
            copy(me, to_peer(i)).wait_send()

    for halos, src in ((k_halos, k_own), (v_halos, v_own)):
        @pl.when(has_next)
        def _():
            for member in range(1, n):
                up(halos, member, src.at[member]).wait_send()

        @pl.when(has_prev)
        def _():
            for member in range(n - 1):
                down(halos, member, src.at[member]).wait_send()


def solution(mesh):
    wide, grp = mesh.shape["wide"], mesh.shape["grp"]
    fold = MOST // grp
    n = fold * grp
    planes = wide // fold

    def body(query_rows, key_rows, value_rows, block_image):
        rows, width = query_rows.shape
        heads = width // HDIM // n
        cols = heads * HDIM
        bf, f32 = jnp.bfloat16, jnp.float32
        vmem = pl.BlockSpec(memory_space=pltpu.VMEM)
        hbm = pl.BlockSpec(memory_space=pl.ANY)
        dma = pltpu.SemaphoreType.DMA
        units = n // 2 * heads
        slices = pltpu.VMEM((n, cols, BLK), bf)
        return pl.pallas_call(
            functools.partial(kernel, (planes, fold, grp, heads)),
            out_shape=jax.ShapeDtypeStruct((rows, width), bf),
            in_specs=[pl.BlockSpec(memory_space=pltpu.SMEM), hbm, hbm, hbm],
            out_specs=vmem,
            scratch_shapes=[pltpu.VMEM((rows, width), bf)] * 3 + [slices] * 6 + [
                pltpu.VMEM((2 * n, cols, BLK), bf),
                pltpu.VMEM((2 * n, cols, BLK), bf),
                pltpu.VMEM((n, heads, BLK, HDIM), bf),
                pltpu.VMEM((2 * n, heads, BLK, HDIM), bf),
                pltpu.VMEM((units, 1, 2 * BLK), f32),
                pltpu.VMEM((units, 1, 2 * BLK), f32),
                pltpu.VMEM((units, HDIM, 2 * BLK), f32),
                pltpu.VMEM((heads, n, BLK, 2 * BLK), f32),
                pltpu.VMEM((units, n * BLK, 2 * BLK), bf),
                pltpu.VMEM((units, n * BLK, 2 * BLK), bf),
                slices, slices,
            ] + [dma((n,))] * 6 + [dma((n,)), dma((n,)), dma((2 * n,))] * 2 + [dma((n,)), dma((n,)), dma((3,))],
            compiler_params=pltpu.CompilerParams(collective_id=0, has_side_effects=True),
        )(block_image, query_rows, key_rows, value_rows)

    return jax.shard_map(
        body,
        mesh=mesh,
        in_specs=(
            P(("wide", "grp"), None),
            P(("wide", "grp"), None),
            P(("wide", "grp"), None),
            P(),
        ),
        out_specs=P(("wide", "grp"), None),
        check_vma=False,
    )
```
